32 devices in a mesh: fer: 4 (over z), bos: 8 (over y, x, core).
Axes of the slice: x: 2, y: 2, z: 4, core: 2. Of those that a mesh axis runs over, the one named last changes fastest.
Arguments:
- green: bfloat16 [4, 32, 9, 64, 128], P(None, 'fer', None, 'bos'), may hold values from -6 to 6
- bos_weight: bfloat16 [64, 9, 64, 128], P('bos'), may hold values from -12 to 12
- vertex: float32 [32, 64], P('fer', 'bos'), may hold values from 0.25 to 1.75
- block_order: int32 [8], replicated, may hold values from 0 to 7, each once
- window_start: int32 [1], replicated, may hold values from 0 to 32
Outputs:
- sigma: float32 [64, 32, 9, 128], P('bos', 'fer')
The draws below stay inside these ranges and needn't reach their ends.
Inputs may be any that keep to these rules, and one draw needn't show every extreme that they name: block_order holds every block number once.
All inputs are finite; a program needn't handle non-finite values.
Results may differ from the reference program's by a relative error of at most 0.0003.
Values may be sent and summed in bfloat16 or wider, within the bound.
No kernel may reach another device: no remote copies, remote signals or barrier semaphores. Data moves between devices by JAX's collectives and lax.ppermute only.
A program may use at most 128 MiB of HBM per device.

```python
import jax
import jax.numpy as jnp
from jax import lax

ORBITAL_COUNT = 3
MOMENTA_FIRST = 64
MOMENTA_SECOND = 64
WB = 8
SLOT_RATIO = 4
WINDOW_FERMIONS = 32
NW = 64
NBLOCKS = 8
SPAN = 32


def block_scale(key, dims, split, least, top_value):
    loudness = 1.0
    for dim, parts in split:
        draws = jax.random.uniform(jax.random.fold_in(jax.random.fold_in(key, 6), dim), (parts,), jnp.float32, least / len(split), top_value / len(split))
        loudness = loudness * jnp.repeat(jnp.exp(draws), dims[dim] // parts).reshape((-1,) + (1,) * (len(dims) - 1 - dim))
    return loudness


def scatter_about(own_key, shape, scale, most, shards=(), held_as=jnp.bfloat16):
    drawn = scale * jax.random.normal(own_key, shape, jnp.float32)
    if shards:
        drawn = drawn * block_scale(own_key, shape, shards, -0.22, 0.18)
    return jnp.clip(drawn, -most, most).astype(held_as)


def setup_inputs(seed: int = 0) -> dict:
    key_of = jax.random.split(jax.random.key(seed), 6)
    green = scatter_about(key_of[0], (SLOT_RATIO, WINDOW_FERMIONS, ORBITAL_COUNT * ORBITAL_COUNT, MOMENTA_FIRST, 2 * MOMENTA_SECOND), 1.0, 6.0, ((1, 4), (3, 8)))
    bos_weight = scatter_about(key_of[1], (NW, ORBITAL_COUNT * ORBITAL_COUNT, MOMENTA_FIRST, 2 * MOMENTA_SECOND), 2.0, 12.0, ((0, 8),))
    vertex = jnp.clip(0.25 + 1.5 * jax.random.uniform(key_of[2], (WINDOW_FERMIONS, NW), jnp.float32) ** block_scale(key_of[2], (WINDOW_FERMIONS, NW), ((0, 4), (1, 8)), -0.2, 0.2), 0.25, 1.75)
    block_order = jax.random.permutation(key_of[3], NBLOCKS).astype(jnp.int32)
    window_start = jax.random.randint(key_of[4], (1,), 0, SPAN + 1).astype(jnp.int32)
    return {"green": green, "bos_weight": bos_weight, "vertex": vertex, "block_order": block_order, "window_start": window_start}


def complex_packed_rows(x):
    return x[..., :MOMENTA_SECOND] + 1j * x[..., MOMENTA_SECOND:]


def reference(green, bos_weight, vertex, block_order, window_start):
    green_complex = complex_packed_rows(green.astype(jnp.float32)).reshape(SLOT_RATIO * WINDOW_FERMIONS, ORBITAL_COUNT * ORBITAL_COUNT, MOMENTA_FIRST, MOMENTA_SECOND)
    start = window_start[0].astype(jnp.int32)
    window = lax.dynamic_slice_in_dim(green_complex, start, WINDOW_FERMIONS + NW, 0)
    green_r = jnp.fft.fft2(window)
    weight_r = jnp.fft.ifft2(complex_packed_rows(bos_weight.astype(jnp.float32)))
    rows = jnp.arange(NW, dtype=jnp.int32)
    omegas = (block_order[rows // WB] * WB + rows % WB).astype(jnp.int32)

    def step(total, item):
        weight_p, omega, column = item
        part = lax.dynamic_slice_in_dim(green_r, omega, WINDOW_FERMIONS, 0).reshape(WINDOW_FERMIONS, ORBITAL_COUNT, ORBITAL_COUNT, MOMENTA_FIRST, MOMENTA_SECOND)
        product = jnp.einsum('nackl,cbkl->nabkl', part, weight_p.reshape(ORBITAL_COUNT, ORBITAL_COUNT, MOMENTA_FIRST, MOMENTA_SECOND))
        return total + column[:, None, None, None, None] * product, None

    zeros = jnp.zeros((WINDOW_FERMIONS, ORBITAL_COUNT, ORBITAL_COUNT, MOMENTA_FIRST, MOMENTA_SECOND), green_r.dtype)
    total, _ = lax.scan(step, zeros, (weight_r, omegas, vertex.T))
    sigma_k = jnp.fft.ifft2(-total.reshape(WINDOW_FERMIONS, ORBITAL_COUNT * ORBITAL_COUNT, MOMENTA_FIRST, MOMENTA_SECOND))
    packed = jnp.concatenate([jnp.real(sigma_k), jnp.imag(sigma_k)], axis=-1)
    return jnp.transpose(packed, (2, 0, 1, 3))
```

```python
import functools
import math

import jax
import jax.numpy as jnp
import numpy as np
from jax import lax
from jax.experimental import pallas as pl
from jax.experimental.pallas import tpu as pltpu
from jax.sharding import PartitionSpec as P

HIGHEST = lax.Precision.HIGHEST
SUBLANES = 8
LANES = 128


def trig_tables(length):
    index = jnp.arange(length, dtype=jnp.int32)
    phase = (index[:, None] * index[None, :] % length).astype(jnp.float32) * (
        2.0 * math.pi / length
    )
    return (jnp.cos(phase), jnp.sin(phase))


def row_matrix(length, forward):
    cosine, sine = trig_tables(length)
    if forward:
        upper = jnp.concatenate([cosine, -sine], axis=1)
        lower = jnp.concatenate([sine, cosine], axis=1)
        block = jnp.concatenate([upper, lower], axis=0)
    else:
        upper = jnp.concatenate([cosine, sine], axis=1)
        lower = jnp.concatenate([-sine, cosine], axis=1)
        block = jnp.concatenate([upper, lower], axis=0) / length
    turned = jnp.concatenate([block[:, length:], -block[:, :length]], axis=1)
    return jnp.concatenate([block, turned], axis=1)


def col_tables(length, forward):
    cosine, sine = trig_tables(length)
    if forward:
        return (cosine, sine)
    return (cosine / length, -sine / length)


def row_step(field, matrix):
    return jnp.einsum("...c,cd->...d", field, matrix, precision=HIGHEST)


def col_step(halves, cos_part, sin_part):
    width = halves.shape[-1] // 2
    first = jnp.einsum("ax,nmxc->nmac", cos_part, halves[..., :width], precision=HIGHEST)
    return first + jnp.einsum("ax,nmxc->nmac", sin_part, halves[..., width:], precision=HIGHEST)


def gathered_body(green, bos_weight, vertex, block_order, window_start):
    num_fer = lax.axis_size("fer")
    fer_index = lax.axis_index("fer")
    bos_index = lax.axis_index("bos")
    num_slot = green.shape[0]
    window_dev = green.shape[1]
    orbitals = int(round(math.sqrt(green.shape[2])))
    bos_dev = bos_weight.shape[0]
    rows_all = bos_weight.shape[2]
    half_width = bos_weight.shape[3] // 2
    block_id = lax.dynamic_index_in_dim(block_order, bos_index, 0, keepdims=False)
    offset = window_start[0] + block_id * bos_dev
    shift_blocks = offset // window_dev
    inner = offset % window_dev
    shift_bits = shift_blocks % num_fer
    forward_rows = row_matrix(half_width, True)
    inverse_rows = row_matrix(half_width, False)
    forward_cos, forward_sin = col_tables(rows_all, True)
    inverse_cos, inverse_sin = col_tables(rows_all, False)
    full_rows = lax.all_gather(green, "bos", axis=3, tiled=True)
    everyone = lax.all_gather(full_rows[None], "fer", axis=0, tiled=True)
    sources = [
        lax.dynamic_index_in_dim(
            everyone, (fer_index + shift_bits + extra) % num_fer, 0, keepdims=False
        )
        for extra in range(3)
    ]
    picked = []
    for extra in range(3):
        slot = (fer_index + shift_blocks + extra) // num_fer % num_slot
        picked.append(lax.dynamic_index_in_dim(sources[extra], slot, 0, keepdims=False))
    blocks = jnp.concatenate(picked, axis=0)
    halves = row_step(blocks.astype(jnp.float32), forward_rows)
    green_real = col_step(halves, forward_cos, forward_sin)
    weight_real = col_step(
        row_step(bos_weight.astype(jnp.float32), inverse_rows), inverse_cos, inverse_sin
    )
    total = jnp.zeros((window_dev, orbitals * orbitals, rows_all, 2 * half_width), jnp.float32)
    for column in range(bos_dev):
        part = lax.dynamic_slice_in_dim(green_real, inner + column, window_dev, 0)
        part = part.reshape(window_dev, orbitals, orbitals, 1, rows_all, 2 * half_width)
        factor = weight_real[column].reshape(1, 1, orbitals, orbitals, rows_all, 2 * half_width)
        green_re, green_im = (part[..., :half_width], part[..., half_width:])
        weight_re, weight_im = (factor[..., :half_width], factor[..., half_width:])
        real_part = jnp.sum(green_re * weight_re - green_im * weight_im, axis=2)
        imag_part = jnp.sum(green_re * weight_im + green_im * weight_re, axis=2)
        product = jnp.concatenate([real_part, imag_part], axis=-1)
        product = product.reshape(window_dev, orbitals * orbitals, rows_all, 2 * half_width)
        total = total + vertex[:, column][:, None, None, None] * product
    sigma_halves = row_step(-total, inverse_rows)
    width = sigma_halves.shape[-1] // 2
    first = jnp.einsum("ax,nmxc->anmc", inverse_cos, sigma_halves[..., :width], precision=HIGHEST)
    return lax.psum_scatter(
        first
        + jnp.einsum("ax,nmxc->anmc", inverse_sin, sigma_halves[..., width:], precision=HIGHEST),
        "bos",
        scatter_dimension=0,
        tiled=True,
    )


def turn(out_index, in_index, length, sign):
    phase = 2.0 * np.pi * (np.multiply.outer(out_index, in_index) % length) / length
    cosine, sine = np.cos(phase), sign * np.sin(phase)
    return np.stack([np.stack([cosine, -sine]), np.stack([sine, cosine])])


@functools.lru_cache(None)
def tables(num_fer, num_bos, rows_all, cols):
    devices = num_fer * num_bos
    near = cols // devices
    kx_dev = rows_all // num_bos
    ry, ky = np.arange(cols), np.arange(cols)
    rx, kx = np.arange(rows_all), np.arange(rows_all)
    eye = np.eye(near)
    t = turn(ry, ky, cols, -1.0)
    to_ry = t.transpose(2, 0, 1, 3).reshape(2 * cols, 2 * cols)
    t = turn(rx, kx, rows_all, -1.0).reshape(2, 2, rows_all, num_bos, kx_dev)
    to_rx = np.einsum("oirbk,nm->bnikomr", t, eye).reshape(
        2 * near * rows_all, 2 * near * rows_all
    )
    t = turn(kx, rx, rows_all, 1.0).reshape(2, 2, num_bos, kx_dev, rows_all)
    to_kx = -np.einsum("oibkr,nm->bnokimr", t, eye).reshape(
        2 * near * rows_all, 2 * near * rows_all
    ) / rows_all
    t = turn(ky, ry, cols, 1.0) / cols
    to_ky = t.transpose(3, 1, 0, 2).reshape(2 * cols, 2 * cols)
    t = turn(ry, ky, cols, 1.0).reshape(2, 2, num_fer, num_bos, near, cols) / cols
    weight_ry = t.transpose(2, 1, 5, 3, 4, 0).reshape(num_fer, 2 * cols, num_bos * near * 2)
    weight_rx = turn(rx, kx, rows_all, 1.0).transpose(3, 1, 0, 2) / rows_all
    out = (to_ry, to_rx, to_kx, to_ky, weight_ry, weight_rx)
    return tuple(np.ascontiguousarray(x, dtype=np.float32) for x in out)


def nt_dot(a, b):
    return lax.dot_general(
        a, b, (((1,), (1,)), ((), ())), precision=HIGHEST, preferred_element_type=jnp.float32
    )


def nn_dot(a, b):
    return lax.dot_general(
        a, b, (((1,), (0,)), ((), ())), precision=HIGHEST, preferred_element_type=jnp.float32
    )


def send_green_kernel(devices, spans, window, start_ref, green_ref, vertex_ref, table_ref, out_ref, rows_ref, part_ref):
    num_slot, held, pairs, kx_dev, width = green_ref.shape
    used = spans * pairs * held
    start = start_ref[0]
    first_slot = start // window
    spill = start % window - lax.axis_index("fer") * held
    for span in range(spans):
        for u in range(held):
            slot = jnp.minimum(first_slot + span + (u < spill).astype(jnp.int32), num_slot - 1)
            block = green_ref[slot, u].astype(jnp.float32)
            base = (span * held + u) * pairs * kx_dev
            rows_ref[pl.ds(base, pairs * kx_dev), :] = block.reshape(pairs * kx_dev, width)
    part_ref[pl.ds(used, part_ref.shape[0] - used), :] = jnp.zeros(
        (part_ref.shape[0] - used, width), jnp.float32
    )
    halves = part_ref.shape[0] // LANES
    blocks = out_ref.shape[0] // (halves * kx_dev)
    for kx in range(kx_dev):
        for span in range(spans):
            for pair in range(pairs):
                base = (span * held * pairs + pair) * kx_dev + kx
                part_ref[pl.ds((span * pairs + pair) * held, held), :] = rows_ref[
                    pl.ds(base, held, stride=pairs * kx_dev), :
                ]
        moved = nt_dot(table_ref[...], part_ref[...])
        for half in range(halves):
            out_ref[pl.ds(half * kx_dev + kx, blocks, stride=halves * kx_dev), :] = moved[
                :, half * LANES : (half + 1) * LANES
            ]
    tile = vertex_ref[...]
    at = used - (halves - 1) * LANES
    for dest in range(devices):
        row = (dest * blocks // devices * halves + halves - 1) * kx_dev
        out_ref[pl.ds(row, held), at : at + tile.shape[1]] = tile


def convolve_kernel(
    num_fer, num_bos, spans, window, start_ref, order_ref, green_ref, weight_ref, to_rx_ref, to_kx_ref,
    out_ref, planes_ref, factor_ref, scale_ref,
):
    held = window // num_fer
    pairs = 9
    bos_dev = weight_ref.shape[0] // (num_bos * 2 * pairs)
    used = spans * pairs * held
    points = LANES
    quads, halves, kx_dev, _ = green_ref.shape
    quads = quads // num_fer
    depth = quads * kx_dev
    start = start_ref[0]
    turn_by = lax.rem(window - start % window, window)
    moved = []
    for fer in range(num_fer):
        turned = []
        for half in range(halves):
            block = green_ref[pl.ds(fer * quads, quads), half].reshape(depth, LANES)
            turned.append(block.T)
        moved.append(nn_dot(jnp.concatenate(turned, axis=0)[:used], to_rx_ref[...]))
    for span in range(spans):
        for pair in range(pairs):
            row = (span * pairs + pair) * held
            both = []
            for part in range(2):
                group = jnp.concatenate(
                    [m[row : row + held, part * points : (part + 1) * points] for m in moved], axis=0
                )
                both.append(pltpu.roll(group, turn_by, 0))
            where = pl.ds(span * window, window)
            planes_ref[pair, where, :] = both[0] + both[1]
            planes_ref[pairs + pair, where, :] = both[0]
            planes_ref[2 * pairs + pair, where, :] = both[1]
    for cb in range(pairs):
        re = weight_ref[pl.ds(2 * cb, num_bos * bos_dev, stride=2 * pairs), :]
        im = weight_ref[pl.ds(2 * cb + 1, num_bos * bos_dev, stride=2 * pairs), :]
        factor_ref[cb] = re
        factor_ref[pairs + cb] = im - re
        factor_ref[2 * pairs + cb] = re + im
    at = used - (halves - 1) * LANES
    for fer in range(num_fer):
        for bos in range(num_bos):
            tile = green_ref[(fer * num_bos + bos) * quads // num_bos, halves - 1, :, at : at + bos_dev]
            for column in range(bos_dev):
                scale_ref[(fer * num_bos + bos) * bos_dev + column] = jnp.broadcast_to(
                    tile[:, column : column + 1], (held, points)
                )
    orbitals = 3
    for fer in range(num_fer):

        def step(p, sums):
            omega = order_ref[p // bos_dev] * bos_dev + p % bos_dev
            where = pl.ds(fer * held + omega, held)
            scale = scale_ref[fer * num_bos * bos_dev + p]
            sums = list(sums)
            for third in range(3):
                g = [planes_ref[third * pairs + pair, where, :] for pair in range(pairs)]
                f = [factor_ref[third * pairs + cb, pl.ds(p, 1), :] * scale for cb in range(pairs)]
                for a in range(orbitals):
                    for b in range(orbitals):
                        value = g[a * orbitals] * f[b]
                        for c in range(1, orbitals):
                            value = value + g[a * orbitals + c] * f[c * orbitals + b]
                        at = third * pairs + a * orbitals + b
                        sums[at] = sums[at] + value
            return tuple(sums)

        zero = jnp.zeros((held, points), jnp.float32)
        sums = lax.fori_loop(0, num_bos * bos_dev, step, (zero,) * (3 * pairs))
        re = jnp.concatenate([sums[i] - sums[2 * pairs + i] for i in range(pairs)], axis=0)
        im = jnp.concatenate([sums[i] + sums[pairs + i] for i in range(pairs)], axis=0)
        sigma = jnp.concatenate([re, im], axis=1)
        out_ref[pl.ds(fer * depth, depth), : pairs * held] = nt_dot(to_kx_ref[...], sigma)


def finish_kernel(held, sum_ref, table_ref, out_ref):
    kx_dev, rows, width = out_ref.shape
    pairs = rows // held
    deep = sum_ref.shape[0] // kx_dev
    for kx in range(kx_dev):
        block = sum_ref[pl.ds(kx, deep, stride=kx_dev), :]
        done = nn_dot(block.T[:rows], table_ref[...])
        for pair in range(pairs):
            out_ref[kx, pl.ds(pair, held, stride=pairs), :] = done[pair * held : (pair + 1) * held]


def real_space_body(green, bos_weight, vertex, block_order, window_start):
    num_fer, num_bos = lax.axis_size("fer"), lax.axis_size("bos")
    devices = num_fer * num_bos
    num_slot, held, pairs, kx_dev, width = green.shape
    bos_dev, _, rows_all, _ = bos_weight.shape
    cols = width // 2
    near = cols // devices
    window = held * num_fer
    spans = -(-(window + num_bos * bos_dev) // window)
    to_ry, to_rx, to_kx, to_ky, weight_ry, weight_rx = tables(num_fer, num_bos, rows_all, cols)
    vmem = pl.BlockSpec(memory_space=pltpu.VMEM)
    smem = pl.BlockSpec(memory_space=pltpu.SMEM)
    lanes = 2 * LANES
    message = pl.pallas_call(
        functools.partial(send_green_kernel, devices, spans, window),
        out_shape=jax.ShapeDtypeStruct((devices * 2 * near * 2 * kx_dev, LANES), jnp.float32),
        in_specs=[smem, vmem, vmem, vmem],
        out_specs=vmem,
        scratch_shapes=[
            pltpu.VMEM((spans * held * pairs * kx_dev, width), jnp.float32),
            pltpu.VMEM((lanes, width), jnp.float32),
        ],
        name="send_green",
    )(window_start, green, vertex, to_ry)
    mine = lax.dynamic_index_in_dim(weight_ry, lax.axis_index("fer"), 0, keepdims=False)
    part = jnp.einsum("pmkc,cd->pmkd", bos_weight.astype(jnp.float32), mine, precision=HIGHEST)
    part = part.reshape(bos_dev, pairs, rows_all, num_bos, near, 2)
    factors = jnp.einsum("pmkbni,kior->bpmonr", part, weight_rx, precision=HIGHEST)
    factors = factors.reshape(num_bos, bos_dev * pairs * 2, near * rows_all)
    factors = lax.all_to_all(factors, "bos", 0, 0, tiled=True)
    message = message.reshape(devices, 2 * near * 2 * kx_dev, LANES)
    message = lax.all_to_all(message, ("fer", "bos"), 0, 0, tiled=True)
    total_rows = devices * 2 * near * kx_dev
    sums = pl.pallas_call(
        functools.partial(convolve_kernel, num_fer, num_bos, spans, window),
        out_shape=jax.ShapeDtypeStruct((total_rows, LANES), jnp.float32),
        in_specs=[smem, smem, vmem, vmem, vmem, vmem],
        out_specs=vmem,
        scratch_shapes=[
            pltpu.VMEM((3 * pairs, spans * window, LANES), jnp.float32),
            pltpu.VMEM((3 * pairs, num_bos * bos_dev, LANES), jnp.float32),
            pltpu.VMEM((num_fer * num_bos * bos_dev, held, LANES), jnp.float32),
        ],
        name="convolve",
    )(
        window_start,
        block_order,
        message.reshape(devices * 2 * near, 2, kx_dev, LANES),
        factors.reshape(num_bos * bos_dev * pairs * 2, LANES),
        to_rx,
        to_kx,
    )
    sums = lax.all_to_all(
        sums.reshape(devices, 2 * near * kx_dev, LANES), ("fer", "bos"), 0, 0, tiled=True
    )
    out = pl.pallas_call(
        functools.partial(finish_kernel, held),
        out_shape=jax.ShapeDtypeStruct((kx_dev, held * pairs, width), jnp.float32),
        in_specs=[vmem, vmem],
        out_specs=vmem,
        name="finish",
    )(sums.reshape(total_rows, LANES), to_ky)
    return out.reshape(kx_dev, held, pairs, width)


def body(green, bos_weight, vertex, block_order, window_start):
    devices = lax.axis_size("fer") * lax.axis_size("bos")
    num_slot, held, pairs, kx_dev, width = green.shape
    bos_dev, _, rows_all, _ = bos_weight.shape
    cols = width // 2
    fits = (
        devices == 32
        and cols % devices == 0
        and (cols // devices) * rows_all == LANES
        and width == LANES
        and pairs == 9
        and held == kx_dev == bos_dev == SUBLANES
    )
    plan = real_space_body if fits else gathered_body
    return plan(green, bos_weight, vertex, block_order, window_start)


def solution(mesh):
    return jax.shard_map(
        body,
        mesh=mesh,
        in_specs=(
            P(None, "fer", None, "bos", None),
            P("bos", None, None, None),
            P("fer", "bos"),
            P(),
            P(),
        ),
        out_specs=P("bos", "fer", None, None),
        check_vma=False,
    )
```

```python
import functools
import math

import jax
import jax.numpy as jnp
import numpy as np
from jax import lax
from jax.experimental import pallas as pl
from jax.experimental.pallas import tpu as pltpu
from jax.sharding import PartitionSpec as P


HIGHEST = lax.Precision.HIGHEST
SUBLANES = 8
LANES = 128


def trig_tables(length):
    index = jnp.arange(length, dtype=jnp.int32)
    phase = (index[:, None] * index[None, :] % length).astype(jnp.float32) * (
        2.0 * math.pi / length
    )
    return (jnp.cos(phase), jnp.sin(phase))


def row_matrix(length, forward):
    cosine, sine = trig_tables(length)
    if forward:
        upper = jnp.concatenate([cosine, -sine], axis=1)
        lower = jnp.concatenate([sine, cosine], axis=1)
        block = jnp.concatenate([upper, lower], axis=0)
    else:
        upper = jnp.concatenate([cosine, sine], axis=1)
        lower = jnp.concatenate([-sine, cosine], axis=1)
        block = jnp.concatenate([upper, lower], axis=0) / length
    turned = jnp.concatenate([block[:, length:], -block[:, :length]], axis=1)
    return jnp.concatenate([block, turned], axis=1)


def col_tables(length, forward):
    cosine, sine = trig_tables(length)
    if forward:
        return (cosine, sine)
    return (cosine / length, -sine / length)


def row_step(field, matrix):
    return jnp.einsum("...c,cd->...d", field, matrix, precision=HIGHEST)


def col_step(halves, cos_part, sin_part):
    width = halves.shape[-1] // 2
    first = jnp.einsum("ax,nmxc->nmac", cos_part, halves[..., :width], precision=HIGHEST)
    return first + jnp.einsum("ax,nmxc->nmac", sin_part, halves[..., width:], precision=HIGHEST)


def gathered_body(green, bos_weight, vertex, block_order, window_start):
    num_fer = lax.axis_size("fer")
    fer_index = lax.axis_index("fer")
    bos_index = lax.axis_index("bos")
    num_slot = green.shape[0]
    window_dev = green.shape[1]
    orbitals = int(round(math.sqrt(green.shape[2])))
    bos_dev = bos_weight.shape[0]
    rows_all = bos_weight.shape[2]
    half_width = bos_weight.shape[3] // 2
    block_id = lax.dynamic_index_in_dim(block_order, bos_index, 0, keepdims=False)
    offset = window_start[0] + block_id * bos_dev
    shift_blocks = offset // window_dev
    inner = offset % window_dev
    shift_bits = shift_blocks % num_fer
    forward_rows = row_matrix(half_width, True)
    inverse_rows = row_matrix(half_width, False)
    forward_cos, forward_sin = col_tables(rows_all, True)
    inverse_cos, inverse_sin = col_tables(rows_all, False)
    full_rows = lax.all_gather(green, "bos", axis=3, tiled=True)
    everyone = lax.all_gather(full_rows[None], "fer", axis=0, tiled=True)
    sources = [
        lax.dynamic_index_in_dim(
            everyone, (fer_index + shift_bits + extra) % num_fer, 0, keepdims=False
        )
        for extra in range(3)
    ]
    picked = []
    for extra in range(3):
        slot = (fer_index + shift_blocks + extra) // num_fer % num_slot
        picked.append(lax.dynamic_index_in_dim(sources[extra], slot, 0, keepdims=False))
    blocks = jnp.concatenate(picked, axis=0)
    halves = row_step(blocks.astype(jnp.float32), forward_rows)
    green_real = col_step(halves, forward_cos, forward_sin)
    weight_real = col_step(
        row_step(bos_weight.astype(jnp.float32), inverse_rows), inverse_cos, inverse_sin
    )
    total = jnp.zeros((window_dev, orbitals * orbitals, rows_all, 2 * half_width), jnp.float32)
    for column in range(bos_dev):
        part = lax.dynamic_slice_in_dim(green_real, inner + column, window_dev, 0)
        part = part.reshape(window_dev, orbitals, orbitals, 1, rows_all, 2 * half_width)
        factor = weight_real[column].reshape(1, 1, orbitals, orbitals, rows_all, 2 * half_width)
        green_re, green_im = (part[..., :half_width], part[..., half_width:])
        weight_re, weight_im = (factor[..., :half_width], factor[..., half_width:])
        real_part = jnp.sum(green_re * weight_re - green_im * weight_im, axis=2)
        imag_part = jnp.sum(green_re * weight_im + green_im * weight_re, axis=2)
        product = jnp.concatenate([real_part, imag_part], axis=-1)
        product = product.reshape(window_dev, orbitals * orbitals, rows_all, 2 * half_width)
        total = total + vertex[:, column][:, None, None, None] * product
    sigma_halves = row_step(-total, inverse_rows)
    width = sigma_halves.shape[-1] // 2
    first = jnp.einsum("ax,nmxc->anmc", inverse_cos, sigma_halves[..., :width], precision=HIGHEST)
    return lax.psum_scatter(
        first
        + jnp.einsum("ax,nmxc->anmc", inverse_sin, sigma_halves[..., width:], precision=HIGHEST),
        "bos",
        scatter_dimension=0,
        tiled=True,
    )


def turn(out_index, in_index, length, sign):
    phase = 2.0 * np.pi * (np.multiply.outer(out_index, in_index) % length) / length
    cosine, sine = np.cos(phase), sign * np.sin(phase)
    return np.stack([np.stack([cosine, -sine]), np.stack([sine, cosine])])


def split_table(table):
    table = table.astype(np.float32)
    high = table.astype(jnp.bfloat16)
    low = (table - high.astype(np.float32)).astype(jnp.bfloat16)
    return np.concatenate([high, low], axis=-1)


@functools.lru_cache(None)
def tables(num_fer, num_bos, rows_all, cols):
    devices = num_fer * num_bos
    near = cols // devices
    kx_dev = rows_all // num_bos
    ry, ky = np.arange(cols), np.arange(cols)
    rx, kx = np.arange(rows_all), np.arange(rows_all)
    eye = np.eye(near)
    t = turn(ry, ky, cols, -1.0)
    to_ry = t.transpose(2, 0, 1, 3).reshape(2 * cols, 2 * cols)
    t = turn(rx, kx, rows_all, -1.0).reshape(2, 2, rows_all, num_bos, kx_dev)
    to_rx = np.einsum("oirbk,nm->bnikomr", t, eye).reshape(
        2 * near * rows_all, 2 * near * rows_all
    )
    t = turn(kx, rx, rows_all, 1.0).reshape(2, 2, num_bos, kx_dev, rows_all)
    to_kx = -np.einsum("oibkr,nm->bnokimr", t, eye).reshape(
        2 * near * rows_all, 2 * near * rows_all
    ) / rows_all
    t = turn(ky, ry, cols, 1.0) / cols
    to_ky = t.transpose(3, 1, 0, 2).reshape(2 * cols, 2 * cols)
    places = LANES // (2 * near * num_bos)
    t = turn(ry, ky, cols, 1.0).reshape(2, 2, num_fer, num_bos, near, cols) / cols
    t = np.einsum("oifbnk,pq->fpikonqb", t, np.eye(places))
    weight_ry = split_table(t.reshape(num_fer, places, 2 * cols, LANES))
    t = turn(rx, kx, rows_all, 1.0) / rows_all
    weight_rx = np.einsum("oirk,nm->inkomr", t, eye).reshape(
        2 * near * rows_all, 2 * near * rows_all
    )
    out = (to_ry, to_rx, to_kx, to_ky, weight_rx)
    return tuple(np.ascontiguousarray(x, dtype=np.float32) for x in out) + (weight_ry,)


def nt_dot(a, b):
    return lax.dot_general(
        a, b, (((1,), (1,)), ((), ())), precision=HIGHEST, preferred_element_type=jnp.float32
    )


def nn_dot(a, b):
    return lax.dot_general(
        a, b, (((1,), (0,)), ((), ())), precision=HIGHEST, preferred_element_type=jnp.float32
    )


def send_green_kernel(devices, spans, window, start_ref, green_ref, vertex_ref, table_ref, out_ref, rows_ref, part_ref):
    num_slot, held, pairs, kx_dev, width = green_ref.shape
    used = spans * pairs * held
    start = start_ref[0]
    first_slot = start // window
    spill = start % window - lax.axis_index("fer") * held
    for span in range(spans):
        for u in range(held):
            slot = jnp.minimum(first_slot + span + (u < spill).astype(jnp.int32), num_slot - 1)
            block = green_ref[slot, u].astype(jnp.float32)
            base = (span * held + u) * pairs * kx_dev
            rows_ref[pl.ds(base, pairs * kx_dev), :] = block.reshape(pairs * kx_dev, width)
    part_ref[pl.ds(used, part_ref.shape[0] - used), :] = jnp.zeros(
        (part_ref.shape[0] - used, width), jnp.float32
    )
    halves = part_ref.shape[0] // LANES
    blocks = out_ref.shape[0] // (halves * kx_dev)
    for kx in range(kx_dev):
        for span in range(spans):
            for pair in range(pairs):
                base = (span * held * pairs + pair) * kx_dev + kx
                part_ref[pl.ds((span * pairs + pair) * held, held), :] = rows_ref[
                    pl.ds(base, held, stride=pairs * kx_dev), :
                ]
        moved = nt_dot(table_ref[...], part_ref[...])
        for half in range(halves):
            out_ref[pl.ds(half * kx_dev + kx, blocks, stride=halves * kx_dev), :] = moved[
                :, half * LANES : (half + 1) * LANES
            ]
    tile = vertex_ref[...]
    at = used - (halves - 1) * LANES
    for dest in range(devices):
        row = (dest * blocks // devices * halves + halves - 1) * kx_dev
        out_ref[pl.ds(row, held), at : at + tile.shape[1]] = tile


def send_weight_kernel(num_bos, weight_ref, to_ry_ref, to_rx_ref, *refs):
    outs, rows_ref = refs[:num_bos], refs[num_bos]
    groups, places, rows_all, width = weight_ref.shape
    fer, me = lax.axis_index("fer"), lax.axis_index("bos")
    both = 0.0
    for place in range(places):
        block = weight_ref[:, place].reshape(groups * rows_all, width)
        both = both + jnp.dot(block, to_ry_ref[fer, place], preferred_element_type=jnp.float32)
    part = both[:, :LANES] + both[:, LANES:]
    turned = []
    deep = places * num_bos
    for group in range(groups):
        block = part[group * rows_all : (group + 1) * rows_all].T
        turned.append(
            jnp.concatenate([block[i * deep : (i + 1) * deep] for i in range(LANES // deep)], axis=1)
        )
    done = nn_dot(jnp.concatenate(turned, axis=0), to_rx_ref[...])
    size = groups * places * 2
    for item in range(groups * places):
        for part in range(2):
            rows_ref[pl.ds(item * 2 + part, num_bos, stride=size), :] = done[
                item * num_bos : (item + 1) * num_bos, part * LANES : (part + 1) * LANES
            ]
    for hop in range(num_bos):
        outs[hop][...] = rows_ref[pl.ds(pl.multiple_of((me ^ hop) * size, SUBLANES), size), :]


def convolve_kernel(
    num_fer, num_bos, spans, window, start_ref, order_ref, green_ref, to_rx_ref, to_kx_ref, *refs
):
    weights, (out_ref, planes_ref, factor_ref, scale_ref) = refs[:num_bos], refs[num_bos:]
    held = window // num_fer
    pairs = 9
    bos_dev = weights[0].shape[0] // (2 * pairs)
    me = lax.axis_index("bos")
    used = spans * pairs * held
    points = LANES
    quads, halves, kx_dev, _ = green_ref.shape
    quads = quads // num_fer
    depth = quads * kx_dev
    start = start_ref[0]
    turn_by = lax.rem(window - start % window, window)
    moved = []
    for fer in range(num_fer):
        turned = []
        for half in range(halves):
            block = green_ref[pl.ds(fer * quads, quads), half].reshape(depth, LANES)
            turned.append(block.T)
        moved.append(nn_dot(jnp.concatenate(turned, axis=0)[:used], to_rx_ref[...]))
    for span in range(spans):
        for pair in range(pairs):
            row = (span * pairs + pair) * held
            both = []
            for part in range(2):
                group = jnp.concatenate(
                    [m[row : row + held, part * points : (part + 1) * points] for m in moved], axis=0
                )
                both.append(pltpu.roll(group, turn_by, 0))
            where = pl.ds(span * window, window)
            planes_ref[pair, where, :] = both[0] + both[1]
            planes_ref[pairs + pair, where, :] = both[0]
            planes_ref[2 * pairs + pair, where, :] = both[1]
    for hop in range(num_bos):
        where = pl.ds(hop * bos_dev, bos_dev)
        for cb in range(pairs):
            re = weights[hop][pl.ds(2 * cb, bos_dev, stride=2 * pairs), :]
            im = weights[hop][pl.ds(2 * cb + 1, bos_dev, stride=2 * pairs), :]
            factor_ref[cb, where, :] = re
            factor_ref[pairs + cb, where, :] = im - re
            factor_ref[2 * pairs + cb, where, :] = re + im
    at = used - (halves - 1) * LANES
    for fer in range(num_fer):
        for bos in range(num_bos):
            tile = green_ref[(fer * num_bos + bos) * quads // num_bos, halves - 1, :, at : at + bos_dev]
            for column in range(bos_dev):
                scale_ref[(fer * num_bos + bos) * bos_dev + column] = jnp.broadcast_to(
                    tile[:, column : column + 1], (held, points)
                )
    orbitals = 3
    for fer in range(num_fer):

        def step(p, sums):
            source = me ^ (p // bos_dev)
            omega = order_ref[source] * bos_dev + p % bos_dev
            where = pl.ds(fer * held + omega, held)
            scale = scale_ref[(fer * num_bos + source) * bos_dev + p % bos_dev]
            sums = list(sums)
            for third in range(3):
                g = [planes_ref[third * pairs + pair, where, :] for pair in range(pairs)]
                f = [factor_ref[third * pairs + cb, pl.ds(p, 1), :] * scale for cb in range(pairs)]
                for a in range(orbitals):
                    for b in range(orbitals):
                        value = g[a * orbitals] * f[b]
                        for c in range(1, orbitals):
                            value = value + g[a * orbitals + c] * f[c * orbitals + b]
                        at = third * pairs + a * orbitals + b
                        sums[at] = sums[at] + value
            return tuple(sums)

        zero = jnp.zeros((held, points), jnp.float32)
        sums = lax.fori_loop(0, num_bos * bos_dev, step, (zero,) * (3 * pairs))
        re = jnp.concatenate([sums[i] - sums[2 * pairs + i] for i in range(pairs)], axis=0)
        im = jnp.concatenate([sums[i] + sums[pairs + i] for i in range(pairs)], axis=0)
        sigma = jnp.concatenate([re, im], axis=1)
        out_ref[pl.ds(fer * depth, depth), : pairs * held] = nt_dot(to_kx_ref[...], sigma)


def finish_kernel(held, sum_ref, table_ref, out_ref):
    kx_dev, pairs, _, _ = out_ref.shape
    rows = pairs * held
    deep = sum_ref.shape[0] // kx_dev
    for kx in range(kx_dev):
        block = sum_ref[pl.ds(kx, deep, stride=kx_dev), :]
        done = nn_dot(block.T[:rows], table_ref[...])
        for pair in range(pairs):
            out_ref[kx, pair] = done[pair * held : (pair + 1) * held]


def real_space_body(green, bos_weight, vertex, block_order, window_start):
    num_fer, num_bos = lax.axis_size("fer"), lax.axis_size("bos")
    devices = num_fer * num_bos
    _, held, pairs, kx_dev, width = green.shape
    bos_dev, _, rows_all, _ = bos_weight.shape
    cols = width // 2
    near = cols // devices
    window = held * num_fer
    spans = -(-(window + num_bos * bos_dev) // window)
    to_ry, to_rx, to_kx, to_ky, weight_rx, weight_ry = tables(num_fer, num_bos, rows_all, cols)
    vmem = pl.BlockSpec(memory_space=pltpu.VMEM)
    smem = pl.BlockSpec(memory_space=pltpu.SMEM)
    lanes = 2 * LANES
    message = pl.pallas_call(
        functools.partial(send_green_kernel, devices, spans, window),
        out_shape=jax.ShapeDtypeStruct((devices * 2 * near * 2 * kx_dev, LANES), jnp.float32),
        in_specs=[smem, vmem, vmem, vmem],
        out_specs=vmem,
        scratch_shapes=[
            pltpu.VMEM((spans * held * pairs * kx_dev, width), jnp.float32),
            pltpu.VMEM((lanes, width), jnp.float32),
        ],
        name="send_green",
    )(window_start, green, vertex, to_ry)
    message = message.reshape(devices, 2 * near * 2 * kx_dev, LANES)
    message, bos_weight = lax.optimization_barrier((message, bos_weight))
    message = lax.all_to_all(message, ("fer", "bos"), 0, 0, tiled=True)
    places = weight_ry.shape[1]
    factors = pl.pallas_call(
        functools.partial(send_weight_kernel, num_bos),
        out_shape=[jax.ShapeDtypeStruct((bos_dev * pairs * 2, LANES), jnp.float32)] * num_bos,
        in_specs=[vmem] * 3,
        out_specs=[vmem] * num_bos,
        scratch_shapes=[pltpu.VMEM((num_bos * bos_dev * pairs * 2, LANES), jnp.float32)],
        cost_estimate=pl.CostEstimate(flops=2 * 10**9, bytes_accessed=3 * 10**6, transcendentals=0),
        name="send_weight",
    )(bos_weight.reshape(bos_dev * pairs // places, places, rows_all, width), weight_ry, weight_rx)
    moved = [factors[0]]
    for hop in range(1, num_bos):
        moved.append(
            lax.ppermute(factors[hop], "bos", [(i, i ^ hop) for i in range(num_bos)])
        )
    total_rows = devices * 2 * near * kx_dev
    sums = pl.pallas_call(
        functools.partial(convolve_kernel, num_fer, num_bos, spans, window),
        out_shape=jax.ShapeDtypeStruct((total_rows, LANES), jnp.float32),
        in_specs=[smem, smem] + [vmem] * (3 + num_bos),
        out_specs=vmem,
        scratch_shapes=[
            pltpu.VMEM((3 * pairs, spans * window, LANES), jnp.float32),
            pltpu.VMEM((3 * pairs, num_bos * bos_dev, LANES), jnp.float32),
            pltpu.VMEM((num_fer * num_bos * bos_dev, held, LANES), jnp.float32),
        ],
        name="convolve",
    )(
        window_start,
        block_order,
        message.reshape(devices * 2 * near, 2, kx_dev, LANES),
        to_rx,
        to_kx,
        *moved,
    )
    sums = lax.all_to_all(
        sums.reshape(devices, 2 * near * kx_dev, LANES), ("fer", "bos"), 0, 0, tiled=True
    )
    out = pl.pallas_call(
        functools.partial(finish_kernel, held),
        out_shape=jax.ShapeDtypeStruct((kx_dev, pairs, held, width), jnp.float32),
        in_specs=[vmem, vmem],
        out_specs=vmem,
        name="finish",
    )(sums.reshape(total_rows, LANES), to_ky)
    return out.transpose(0, 2, 1, 3)


def body(green, bos_weight, vertex, block_order, window_start):
    devices = lax.axis_size("fer") * lax.axis_size("bos")
    _, held, pairs, kx_dev, width = green.shape
    bos_dev, _, rows_all, _ = bos_weight.shape
    cols = width // 2
    fits = (
        devices == 32
        and cols % devices == 0
        and (cols // devices) * rows_all == LANES
        and width == LANES
        and pairs == 9
        and held == kx_dev == bos_dev == SUBLANES
        and lax.axis_size("bos") & (lax.axis_size("bos") - 1) == 0
    )
    if not fits:
        return gathered_body(green, bos_weight, vertex, block_order, window_start)
    return real_space_body(green, bos_weight, vertex, block_order, window_start)


def solution(mesh):
    return jax.shard_map(
        body,
        mesh=mesh,
        in_specs=(
            P(None, "fer", None, "bos", None),
            P("bos", None, None, None),
            P("fer", "bos"),
            P(),
            P(),
        ),
        out_specs=P("bos", "fer", None, None),
        check_vma=False,
    )
```
